32 devices in a mesh: dp: 16 (over z, y, x), mp: 2 (over core).
Axes of the slice: x: 2, y: 2, z: 4, core: 2. Of those that a mesh axis runs over, the one named last changes fastest.
Arguments:
- grads: bfloat16 [16384, 16384], P('dp', 'mp'), may hold values from -6 to 6
- scales: float32 [128, 16384], P('mp', 'dp'), may hold values from 0.25 to 4
- example_group: int32 [16, 1024], P('dp'), may hold values from 0 to 127, never falling along the last dimension, each value on 1 to 32 neighbouring positions
- group_slot: int32 [2048], P('dp'), may hold values from 0 to 2047, as said below
- inv_hess: bfloat16 [16384, 16384], P('mp', 'dp'), may hold values from -0.046875 to 0.046875
- queries: bfloat16 [512, 16384], P(None, 'mp'), may hold values from -0.029907227 to 0.029907227
Outputs:
- scores: float32 [2048, 512], P('dp', 'mp')
The draws below stay inside these ranges and needn't reach their ends.
Inputs may be any that keep to these rules, and one draw needn't show every extreme that they name: `group_slot`: A permutation of the 2048 rows. The groups of one block of 128 (one index of dp) put at most 16 groups into the rows of any one owner block of 128 output rows, and exactly 16 into some owner block.
All inputs are finite; a program needn't handle non-finite values.
Results may differ from the reference program's by a relative error of at most 0.0049.
Values may be sent and summed in bfloat16 or wider, within the bound.
No kernel may reach another device: no remote copies, remote signals or barrier semaphores. Data moves between devices by JAX's collectives and lax.ppermute only.
A program may use at most 128 MiB of HBM per device.

```python
import math
import jax
import jax.numpy as jnp
import numpy as np
from jax import lax

P_SIZE = 16384
QBLOCK = 128
GRP_DEV = 128
EX_DEV = 1024
GROUPS = 2048
EXAMPLES = 16384
NQ = 512
N_DP = 16


def draw_group_slot(key, part):
    per_owner = GRP_DEV // N_DP
    first, second = jax.random.split(jax.random.fold_in(key, 11))
    leading = jax.random.permutation(first, N_DP)
    trailing = jnp.roll(leading, -1)
    owners = jnp.arange(N_DP, dtype=jnp.int32)
    counts = per_owner + per_owner * (owners[None, :] == leading[:, None]).astype(jnp.int32) - per_owner * (owners[None, :] == trailing[:, None]).astype(jnp.int32)
    ends = jnp.cumsum(counts, axis=1)
    starts = ends - counts
    offsets = jnp.cumsum(counts, axis=0) - counts
    row_keys = jax.random.split(second, N_DP)
    shuffles = jax.vmap(lambda one_key: jax.random.permutation(one_key, GRP_DEV))(row_keys)
    position = jnp.arange(GRP_DEV, dtype=jnp.int32)
    target = jnp.sum((position[None, :, None] >= ends[:, None, :]).astype(jnp.int32), axis=2)
    within = position[None, :] - jnp.take_along_axis(starts, target, axis=1)
    slot_at = target * GRP_DEV + jnp.take_along_axis(offsets, target, axis=1) + within
    placing = jnp.argsort(shuffles, axis=1)
    by_group = jnp.take_along_axis(slot_at, placing, axis=1)
    return by_group.reshape(-1).astype(jnp.int32)


def block_scale(own_key, dims, shards, low, high):
    def one(dim, blocks):
        steps = jax.random.uniform(jax.random.fold_in(jax.random.fold_in(own_key, 6), dim), (blocks,), jnp.float32, low / len(shards), high / len(shards))
        return jnp.repeat(jnp.exp(steps), dims[dim] // blocks).reshape((-1,) + (1,) * (len(dims) - dim - 1))

    factor_of = one(*shards[0])
    for cut in shards[1:]:
        factor_of = factor_of * one(*cut)
    return factor_of


def split_up(amount, total, most, lean):
    weights = [(1 << 20) // math.isqrt(standing ** lean) + 1 for standing in range(2, amount + 1)]
    spare, given = total - most - (amount - 1), [1] * (amount - 1)
    while spare > 0:
        candidates = [i for i in range(amount - 1) if given[i] < most]
        pool, remaining = sum([weights[i] for i in candidates]), spare
        for i in candidates:
            addition = min(most - given[i], max(1, remaining * weights[i] // pool), spare)
            given[i] = given[i] + addition
            spare = spare - addition
    return np.array([most] + given)


def uneven_parts(key, amount, total, reach, skew):
    if amount == 2:
        one = jax.random.randint(key, (), max(1, total - reach), min(reach, total - 1) + 1)
        return jnp.stack([one, total - one])
    lengths = jnp.asarray(split_up(amount, total, reach, skew), jnp.int32)
    couples = (amount - 1) // 2
    source_of, sink = lengths[1:1 + 2 * couples:2], lengths[2:2 + 2 * couples:2]
    margin = jnp.minimum(source_of - 1, reach - sink)
    passed = jax.random.randint(jax.random.fold_in(key, 1), (couples,), 0, 1 << 20) % (margin + 1)
    lengths = lengths.at[1:1 + 2 * couples:2].set(source_of - passed).at[2:2 + 2 * couples:2].set(sink + passed)
    return lengths[jax.random.permutation(jax.random.fold_in(key, 2), amount)]


def centred(rng, dims, spread, reach, cuts=(), held_as=jnp.bfloat16):
    array = spread * jax.random.normal(rng, dims, jnp.float32)
    if cuts:
        array = array * block_scale(rng, dims, cuts, -0.22, 0.18)
    return jnp.clip(array, -reach, reach).astype(held_as)


def setup_inputs(seed: int = 0) -> dict:
    seeds = jax.random.split(jax.random.key(seed), 7)
    grads = centred(seeds[0], (EXAMPLES, P_SIZE), 1.0, 6.0, ((0, 16), (1, 2)))
    scales = jnp.clip(jnp.exp(math.log(4.0) - 2.7725887 * jax.random.uniform(seeds[1], (P_SIZE // QBLOCK, EXAMPLES), jnp.float32) ** block_scale(seeds[1], (P_SIZE // QBLOCK, EXAMPLES), ((0, 2), (1, 16)), -0.2, 0.2)), 0.25, 4.0)
    example_group = jax.vmap(lambda own: jnp.searchsorted(jnp.cumsum(uneven_parts(own, GRP_DEV, EX_DEV, 4 * EX_DEV // GRP_DEV, 2)), jnp.arange(EX_DEV), side="right"))(jax.random.split(seeds[2], N_DP)).reshape((N_DP, EX_DEV)).astype(jnp.int32)
    group_slot = draw_group_slot(jax.random.fold_in(seeds[6], 71), 0)
    inv_hess = centred(seeds[4], (P_SIZE, P_SIZE), P_SIZE ** -0.5, 0.046875, ((0, 2), (1, 16)))
    queries = centred(seeds[5], (NQ, P_SIZE), 0.005, 0.029907227, ((1, 2),))
    return {"grads": grads, "scales": scales, "example_group": example_group, "group_slot": group_slot, "inv_hess": inv_hess, "queries": queries}


def block_sums(pieces):
    rows, block_scales, members = pieces
    dequant = (rows.reshape(EX_DEV, P_SIZE // QBLOCK, QBLOCK) * jnp.transpose(block_scales)[:, :, None]).astype(jnp.bfloat16).reshape(EX_DEV, P_SIZE)
    onehot = (jnp.arange(GRP_DEV, dtype=jnp.int32)[:, None] == members[None, :]).astype(jnp.bfloat16)
    return jnp.dot(onehot, dequant, preferred_element_type=jnp.float32).astype(jnp.bfloat16)


def reference(grads, scales, example_group, group_slot, inv_hess, queries):
    grad_blocks = grads.reshape(N_DP, EX_DEV, P_SIZE)
    scale_blocks = jnp.transpose(scales.reshape(P_SIZE // QBLOCK, N_DP, EX_DEV), (1, 0, 2))
    group_grad = lax.map(block_sums, (grad_blocks, scale_blocks, example_group)).reshape(GROUPS, P_SIZE)
    precond = jnp.dot(queries, inv_hess, preferred_element_type=jnp.float32).astype(jnp.bfloat16)
    raw = lax.dot_general(group_grad, precond, (((1,), (1,)), ((), ())), preferred_element_type=jnp.float32)
    scores = jnp.zeros((GROUPS, NQ), jnp.float32).at[group_slot.astype(jnp.int32)].set(raw)
    return scores
```

```python
import jax
import jax.numpy as jnp
from jax import lax
from jax.experimental import pallas as pl
from jax.experimental.pallas import tpu as pltpu
from jax.sharding import PartitionSpec as P

QBLOCK = 128
GRP_DEV = 128
AXES = ("dp", "mp")
LANES = 128
TAG = 16


def params(*semantics):
    return pltpu.CompilerParams(dimension_semantics=semantics)


def precond_kernel(place, queries, inv_hess, mine, theirs, left, right, acc, sems, *, cut, blocks):
    width = right.shape[1]
    copies = []
    start = 0
    for i, depth in enumerate(blocks):
        span = pl.ds(start, depth)
        pair = (
            pltpu.make_async_copy(queries.at[:, span], left.at[:, span], sems.at[0, i]),
            pltpu.make_async_copy(
                inv_hess.at[span, pl.ds(cut * width, width)], right.at[span, :], sems.at[1, i]
            ),
        )
        for copy in pair:
            copy.start()
        copies.append((span, pair))
        start += depth
    for i, (span, pair) in enumerate(copies):
        for copy in pair:
            copy.wait()
        product = jnp.dot(left[:, span], right[span, :], preferred_element_type=jnp.float32)
        if i == 0:
            acc[...] = product
        else:
            acc[...] += product
    lane, share = place[2], mine.shape[0]
    mine[...] = acc[pl.ds(lane * share, share), :]
    for other in range(theirs.shape[0]):
        first = jnp.bitwise_xor(lane, other + 1) * share
        theirs[other] = acc[pl.ds(first, share), :]


def precond_part(place, queries, inv_hess, lanes, cut, cuts):
    count, depth = queries.shape
    width = inv_hess.shape[1] // cuts
    share = count // lanes
    unit = depth // 16
    blocks = (unit, unit, 2 * unit, 4 * unit, 4 * unit, 4 * unit)
    whole = pl.BlockSpec(memory_space=pl.ANY)
    return pl.pallas_call(
        lambda *refs: precond_kernel(*refs, cut=cut, blocks=blocks),
        grid_spec=pltpu.PrefetchScalarGridSpec(
            num_scalar_prefetch=1,
            grid=(1,),
            in_specs=[whole, whole],
            out_specs=[
                pl.BlockSpec((share, width), lambda k, _: (0, 0)),
                pl.BlockSpec((lanes - 1, share, width), lambda k, _: (0, 0, 0)),
            ],
            scratch_shapes=[
                pltpu.VMEM((count, depth), queries.dtype),
                pltpu.VMEM((depth, width), inv_hess.dtype),
                pltpu.VMEM((count, width), jnp.float32),
                pltpu.SemaphoreType.DMA((2, len(blocks))),
            ],
        ),
        out_shape=[
            jax.ShapeDtypeStruct((share, width), jnp.float32),
            jax.ShapeDtypeStruct((lanes - 1, share, width), jnp.float32),
        ],
        compiler_params=params("arbitrary"),
        cost_estimate=pl.CostEstimate(
            flops=2 * count * depth * width,
            transcendentals=0,
            bytes_accessed=2 * (count * depth + depth * width),
        ),
    )(place, queries, inv_hess)


def group_kernel(
    place, grads, scales, onehot, tag, out, buffer, sems, *, peer, chips, columns, width, cut
):
    rows = buffer.shape[0]
    groups = onehot.shape[0]
    blocks = cut // QBLOCK
    copies = []
    for c in range(columns):
        column = c * chips + jnp.bitwise_xor(place[1], peer)
        for start in range(0, width, cut):
            at = c * width + start
            copy = pltpu.make_async_copy(
                grads.at[:, pl.ds(pl.multiple_of(column * width + start, LANES), cut)],
                buffer.at[:, pl.ds(at, cut)],
                sems.at[len(copies)],
            )
            copy.start()
            copies.append((copy, at, column, start // QBLOCK))
    out[groups:, :] = jnp.zeros((TAG, out.shape[1]), jnp.bfloat16)
    out[groups:, : tag.shape[1]] = tag[...]
    for copy, at, column, first in copies:
        copy.wait()
        turned = buffer[:, at : at + cut].T.astype(jnp.float32).reshape(blocks, QBLOCK, rows)
        steps = scales[column][first : first + blocks, :]
        dequant = (turned * steps[:, None, :]).astype(jnp.bfloat16).reshape(cut, rows)
        out[:groups, at : at + cut] = lax.dot_general(
            onehot[...], dequant, (((1,), (1,)), ((), ())), preferred_element_type=jnp.float32
        ).astype(jnp.bfloat16)


def group_part(place, grads, scales, onehot, tag, peer, chips, columns, width):
    rows = grads.shape[0]
    groups = onehot.shape[0]
    cut = min(512, width)
    scales = scales.reshape(-1, width // QBLOCK, rows)
    return pl.pallas_call(
        lambda *refs: group_kernel(
            *refs, peer=peer, chips=chips, columns=columns, width=width, cut=cut
        ),
        grid_spec=pltpu.PrefetchScalarGridSpec(
            num_scalar_prefetch=1,
            grid=(1,),
            in_specs=[
                pl.BlockSpec(memory_space=pl.ANY),
                pl.BlockSpec(scales.shape, lambda c, _: (0, 0, 0)),
                pl.BlockSpec(onehot.shape, lambda c, _: (0, 0)),
                pl.BlockSpec(tag.shape, lambda c, _: (0, 0)),
            ],
            out_specs=pl.BlockSpec((groups + TAG, columns * width), lambda c, _: (0, 0)),
            scratch_shapes=[
                pltpu.VMEM((rows, columns * width), grads.dtype),
                pltpu.SemaphoreType.DMA((columns * width // cut,)),
            ],
        ),
        out_shape=jax.ShapeDtypeStruct((groups + TAG, columns * width), jnp.bfloat16),
        compiler_params=params("arbitrary"),
        cost_estimate=pl.CostEstimate(
            flops=2 * groups * rows * columns * width,
            transcendentals=0,
            bytes_accessed=2 * rows * columns * width,
        ),
    )(place, grads, scales, onehot, tag)


def near_kernel(place, *refs, chips, lanes, per_lane, cuts):
    routing, refs = refs[0], refs[1:]
    pieces, refs = refs[: chips * lanes], refs[chips * lanes :]
    out, far, left, total = refs[-4:]
    precond = refs[:-4]
    step, steps = pl.program_id(0), pl.num_programs(0)
    groups = pieces[0].shape[0] - TAG
    source = jnp.bitwise_xor(place[0], step) // per_lane
    holder = jnp.bitwise_xor(source, place[2])
    for lane in range(lanes):

        @pl.when(holder == lane)
        def _():
            for chip in range(chips):
                piece = pieces[lane * chips + chip]
                left[chip * groups : (chip + 1) * groups, :] = piece[:groups, :]

    width = left.shape[1] // cuts
    for hop in range(len(precond) // cuts):

        @pl.when(step == hop)
        def _():
            value = None if hop == 0 else total[...]
            for cut in range(cuts):
                part = lax.dot_general(
                    left[:, cut * width : (cut + 1) * width],
                    precond[hop * cuts + cut][...],
                    (((1,), (1,)), ((), ())),
                    preferred_element_type=jnp.float32,
                )
                value = part if value is None else value + part
            total[...] = value

    @pl.when(step == steps - 1)
    def _():
        far[...] = jnp.dot(
            routing[...], left[...], preferred_element_type=jnp.float32
        ).astype(jnp.bfloat16)
        high = total[...].astype(jnp.bfloat16)
        low = (total[...] - high.astype(jnp.float32)).astype(jnp.bfloat16)
        out[...] = jnp.dot(routing[...], high, preferred_element_type=jnp.float32) + jnp.dot(
            routing[...], low, preferred_element_type=jnp.float32
        )


def near_part(place, routing, pieces, precond, chips, lanes, per_lane, cuts):
    share, width = precond[0].shape
    width = width * cuts
    groups = pieces[0].shape[0] - TAG
    rows = chips * groups
    steps = len(precond) // cuts + 1
    sent = routing.shape[0]

    def column(i, at):
        return (0, jnp.bitwise_xor(at[0], i) % per_lane)

    return pl.pallas_call(
        lambda *refs: near_kernel(
            *refs, chips=chips, lanes=lanes, per_lane=per_lane, cuts=cuts
        ),
        grid_spec=pltpu.PrefetchScalarGridSpec(
            num_scalar_prefetch=1,
            grid=(steps,),
            in_specs=[pl.BlockSpec(routing.shape, lambda i, at: (0, 0))]
            + [pl.BlockSpec((groups + TAG, width), column) for _ in pieces]
            + [pl.BlockSpec(p.shape, lambda i, at: (0, 0)) for p in precond],
            out_specs=[
                pl.BlockSpec((sent, share), lambda i, at: (0, 0)),
                pl.BlockSpec((sent, width), lambda i, at: (0, 0)),
            ],
            scratch_shapes=[
                pltpu.VMEM((rows, width), jnp.bfloat16),
                pltpu.VMEM((rows, share), jnp.float32),
            ],
        ),
        out_shape=[
            jax.ShapeDtypeStruct((sent, share), jnp.float32),
            jax.ShapeDtypeStruct((sent, width), jnp.bfloat16),
        ],
        compiler_params=params("arbitrary"),
        cost_estimate=pl.CostEstimate(
            flops=2 * rows * width * share * (steps - 1),
            transcendentals=0,
            bytes_accessed=2 * rows * width * steps * lanes,
        ),
        name="near",
    )(place, routing, *pieces, *precond)


def local(grads, scales, example_group, group_slot, inv_hess, queries):
    devices = lax.axis_size("dp")
    lanes = lax.axis_size("mp")
    chips = 1 << ((devices.bit_length() - 1) // 2)
    line = devices // chips
    per_lane = line // lanes
    width = inv_hess.shape[1]
    share = queries.shape[0] // lanes
    capacity = 2 * GRP_DEV // devices
    at_line = lax.axis_index("dp") // chips
    at_plane = lax.axis_index("dp") % chips
    place = jnp.stack([at_line, at_plane, lax.axis_index("mp")]).astype(jnp.int32)
    cuts = 1

    def move(value, target):
        pairs = []
        for s in range(line):
            for t in range(chips):
                for m in range(lanes):
                    to = target(s, t, m)
                    if to is not None:
                        a, b, c = to
                        pairs.append(((s * chips + t) * lanes + m, (a * chips + b) * lanes + c))
        return lax.ppermute(value, AXES, pairs)

    def to_lane(value, hop):
        return move(value, lambda s, t, m: (s, t, m ^ hop))

    def to_plane(value, hop):
        return move(value, lambda s, t, m: (s, t ^ hop, m))

    def to_line(value, hop):
        return move(value, lambda s, t, m: (s ^ hop, t, m))

    nearer, farthest = [[] for _ in range(line - 1)], []
    for cut in range(cuts):
        mine, theirs = precond_part(place, queries, inv_hess, lanes, cut, cuts)
        block = mine
        for hop in range(1, lanes):
            block = block + to_lane(theirs[hop - 1], hop)
        block = block.astype(jnp.bfloat16)
        nearer[0].append(block)
        if line == 4:
            two = to_line(block, 2)
            one = to_line(block, 1)
            middle = move(block, lambda s, t, m: (s ^ 3, t, m) if s in (1, 2) else None)
            relayed = move(two, lambda s, t, m: (s ^ 1, t, m) if s in (1, 2) else None)
            nearer[1].append(one)
            nearer[2].append(two)
            farthest.append(middle + relayed)
        else:
            for hop in range(1, line - 1):
                nearer[hop].append(to_line(block, hop))
            farthest.append(to_line(block, line - 1))

    slot = group_slot.reshape(1, GRP_DEV)
    tag = jnp.concatenate([slot // GRP_DEV, slot % GRP_DEV], axis=0)
    tag = jnp.pad(tag, ((0, TAG - 2), (0, 0))).astype(jnp.bfloat16)
    onehot = (
        jnp.arange(GRP_DEV, dtype=jnp.int32)[:, None] == example_group[0][None, :]
    ).astype(jnp.bfloat16)
    pieces = []
    for hop in [*range(chips - 1, 0, -1), 0]:
        made = group_part(place, grads, scales, onehot, tag, hop, chips, per_lane, width)
        pieces.append(to_plane(made, hop) if hop else made)
    pieces = pieces[::-1]
    held = list(pieces)
    for hop in range(1, lanes):
        held += [to_lane(piece, hop) for piece in pieces]

    tags = jnp.stack([p[GRP_DEV : GRP_DEV + 2, :GRP_DEV] for p in pieces]).astype(jnp.int32)
    owner, inside = tags[:, 0], tags[:, 1]
    source = jnp.bitwise_xor(jnp.arange(chips, dtype=jnp.int32), at_plane)[:, None]
    order = jnp.arange(GRP_DEV, dtype=jnp.int32)
    earlier = (owner[:, :, None] == owner[:, None, :]) & (order[None, :] < order[:, None])[None]
    rank = jnp.sum(earlier.astype(jnp.int32), axis=2)
    per_chip = chips * line * capacity
    toward = jnp.bitwise_xor(owner % chips, at_plane)
    row = toward * per_chip + (source * line + owner // chips) * capacity + rank
    rows = jnp.arange(chips * per_chip, dtype=jnp.int32)[:, None]
    routing = (rows == row.reshape(1, -1)).astype(jnp.bfloat16)
    kept = rows[:per_chip] == row.reshape(1, -1)
    meta = GRP_DEV + jnp.sum(
        jnp.where(kept, inside.reshape(1, -1) - GRP_DEV, 0), axis=1, keepdims=True
    )
    meta = jnp.broadcast_to(meta, (per_chip, LANES)).astype(jnp.bfloat16)
    meta = meta.reshape(chips, line, capacity, LANES)

    total, far = near_part(
        place, routing, held, sum(nearer, []), chips, lanes, per_lane, cuts
    )
    for cut in range(cuts):
        columns = slice(cut * width // cuts, (cut + 1) * width // cuts)
        total = total + contract(far[:, columns], farthest[cut])
    sending = total.astype(jnp.bfloat16).reshape(chips, per_chip, share)
    whole = sending[0].astype(jnp.float32)
    for hop in range(1, chips):
        whole = whole + to_plane(sending[hop], hop).astype(jnp.float32)
    whole = whole.astype(jnp.bfloat16).reshape(chips, line, capacity, share)
    whole = jnp.concatenate([whole, meta], axis=3)
    final = []
    for hop in range(line):
        own = lax.dynamic_index_in_dim(whole, jnp.bitwise_xor(at_line, hop), 1, keepdims=False)
        own = own.reshape(chips * capacity, share + LANES)
        final.append(to_line(own, hop) if hop else own)
    final = jnp.concatenate(final, axis=0)
    chosen = (final[:, share:] == jnp.arange(LANES, dtype=jnp.bfloat16)[None, :]).astype(
        jnp.bfloat16
    )
    return lax.dot_general(
        chosen, final[:, :share], (((0,), (0,)), ((), ())), preferred_element_type=jnp.float32
    )


def contract(left, right):
    return lax.dot_general(
        left, right, (((1,), (1,)), ((), ())), preferred_element_type=jnp.float32
    )


def solution(mesh):
    in_specs = (P("dp", "mp"), P("mp", "dp"), P("dp", None), P("dp"), P("mp", "dp"), P(None, "mp"))
    out_specs = P("dp", "mp")

    return jax.shard_map(local, mesh=mesh, in_specs=in_specs, out_specs=out_specs, check_vma=False)
```

```python
import jax
import jax.numpy as jnp
from jax import lax
from jax.experimental import pallas as pl
from jax.experimental.pallas import tpu as pltpu
from jax.sharding import PartitionSpec as P

QBLOCK = 128
GRP_DEV = 128
AXES = ("dp", "mp")
LANES = 128


ANYWHERE = pl.BlockSpec(memory_space=pl.ANY)
ON_CHIP = pl.BlockSpec(memory_space=pltpu.VMEM)


def room(*sizes):
    return pltpu.CompilerParams(vmem_limit_bytes=sum(sizes) + (4 << 20))


def on_chip(value):
    return pltpu.with_memory_space_constraint(value, pltpu.VMEM)


def precond_kernel(queries, inv_hess, mine, *refs, cut, blocks):
    theirs, (left, right, acc, sems) = refs[:-4], refs[-4:]
    width = right.shape[1]
    copies = []
    start = 0
    for i, depth in enumerate(blocks):
        span = pl.ds(start, depth)
        pair = (
            pltpu.make_async_copy(queries.at[:, span], left.at[:, span], sems.at[0, i]),
            pltpu.make_async_copy(
                inv_hess.at[span, pl.ds(cut * width, width)], right.at[span, :], sems.at[1, i]
            ),
        )
        for copy in pair:
            copy.start()
        copies.append((span, pair))
        start += depth
    for i, (span, pair) in enumerate(copies):
        for copy in pair:
            copy.wait()
        product = jnp.dot(left[:, span], right[span, :], preferred_element_type=jnp.float32)
        if i == 0:
            acc[...] = product
        else:
            acc[...] += product
    lane, share = lax.axis_index("mp"), mine.shape[0]
    mine[...] = acc[pl.ds(lane * share, share), :]
    for other, out in enumerate(theirs):
        first = jnp.bitwise_xor(lane, other + 1) * share
        out[...] = acc[pl.ds(first, share), :]


def precond_part(queries, inv_hess, lanes, cut, cuts):
    count, depth = queries.shape
    width = inv_hess.shape[1] // cuts
    share = count // lanes
    unit = depth // 16
    blocks = (unit, unit, 2 * unit, 4 * unit, 4 * unit, 4 * unit)
    return pl.pallas_call(
        lambda *refs: precond_kernel(*refs, cut=cut, blocks=blocks),
        in_specs=[ANYWHERE, ANYWHERE],
        out_specs=[ON_CHIP] * lanes,
        scratch_shapes=[
            pltpu.VMEM((count, depth), queries.dtype),
            pltpu.VMEM((depth, width), inv_hess.dtype),
            pltpu.VMEM((count, width), jnp.float32),
            pltpu.SemaphoreType.DMA((2, len(blocks))),
        ],
        out_shape=[pltpu.VMEM((share, width), jnp.float32)] * lanes,
        cost_estimate=pl.CostEstimate(
            flops=2 * count * depth * width,
            transcendentals=0,
            bytes_accessed=2 * (count * depth + depth * width),
        ),
        name="precond",
    )(queries, inv_hess)


def group_kernel(grads, scales, onehot, *refs, peers, chips, columns, width):
    outs, buffer, sems = refs[:-2], refs[-2], refs[-1]
    rows = buffer.shape[1]
    blocks = width // QBLOCK
    copies = []
    for out, peer in zip(outs, peers):
        for c in range(columns):
            column = c * chips + jnp.bitwise_xor(lax.axis_index("dp") % chips, peer)
            copy = pltpu.make_async_copy(
                grads.at[:, pl.ds(pl.multiple_of(column * width, width), width)],
                buffer.at[len(copies)],
                sems.at[len(copies)],
            )
            copy.start()
            copies.append((copy, out, column, c * width))
    for i, (copy, out, column, at) in enumerate(copies):
        copy.wait()
        turned = buffer[i].T.astype(jnp.float32).reshape(blocks, QBLOCK, rows)
        dequant = (turned * scales[column][:, None, :]).astype(jnp.bfloat16).reshape(width, rows)
        out[:, at : at + width] = lax.dot_general(
            onehot[...], dequant, (((1,), (1,)), ((), ())), preferred_element_type=jnp.float32
        ).astype(jnp.bfloat16)


def group_part(grads, scales, onehot, peers, chips, columns, width):
    rows = grads.shape[0]
    groups = onehot.shape[0]
    scales = scales.reshape(-1, width // QBLOCK, rows)
    shape = (groups, columns * width)
    count = len(peers) * columns
    return pl.pallas_call(
        lambda *refs: group_kernel(
            *refs, peers=peers, chips=chips, columns=columns, width=width
        ),
        in_specs=[ANYWHERE, ON_CHIP, ON_CHIP],
        out_specs=[ON_CHIP for _ in peers],
        scratch_shapes=[
            pltpu.VMEM((count, rows, width), grads.dtype),
            pltpu.SemaphoreType.DMA((count,)),
        ],
        out_shape=[pltpu.VMEM(shape, jnp.bfloat16) for _ in peers],
        cost_estimate=pl.CostEstimate(
            flops=2 * groups * rows * count * width,
            transcendentals=0,
            bytes_accessed=2 * rows * count * width,
        ),
    )(grads, on_chip(scales), on_chip(onehot))


def hop_of(pair):
    at_end, between = pair
    if at_end == between:
        return at_end, True
    where = lax.axis_index("dp") // (lax.axis_size("dp") // 4)
    inside = (where == 1) | (where == 2)
    if at_end is None:
        return between, inside
    if between is None:
        return at_end, jnp.logical_not(inside)
    return jnp.where(inside, between, at_end), True


def when(condition):
    return (lambda body: body()) if condition is True else pl.when(condition)


def near_kernel(*refs, hops, late, chips, lanes, per_lane, plane):
    pieces, refs = refs[: chips * lanes], refs[chips * lanes :]
    precond, total, left = refs[: len(hops)], refs[len(hops)], refs[-1]
    fars = refs[len(hops) + 1 : -1]
    rows, width = left.shape
    groups = rows // chips
    at_line = lax.axis_index("dp") // plane

    def lay(target, hop):
        source = jnp.bitwise_xor(at_line, hop)
        holder = jnp.bitwise_xor(source // per_lane, lax.axis_index("mp"))
        inner = source % per_lane
        for lane in range(lanes):
            for k in range(per_lane):

                @pl.when((holder == lane) & (inner == k))
                def _():
                    for chip in range(chips):
                        target[chip * groups : (chip + 1) * groups, :] = pieces[
                            lane * chips + chip
                        ][:groups, k * width : (k + 1) * width]

    for i, (pair, block) in enumerate(zip(hops, precond)):
        hop, here = hop_of(pair)

        @when(here)
        def _():
            lay(left, hop)
            part = contract(left[...], block[...])
            total[...] = part if i == 0 else total[...] + part

    for pair, far in zip(late, fars):
        hop, here = hop_of(pair)
        when(here)(lambda: lay(far, hop))


def near_part(pieces, precond, hops, late, chips, lanes, per_lane, plane):
    share, width = precond[0].shape
    rows = chips * (pieces[0].shape[0])
    return pl.pallas_call(
        lambda *refs: near_kernel(
            *refs,
            hops=hops,
            late=late,
            chips=chips,
            lanes=lanes,
            per_lane=per_lane,
            plane=plane,
        ),
        in_specs=[ON_CHIP] * (len(pieces) + len(precond)),
        out_specs=[ON_CHIP] * (1 + len(late)),
        scratch_shapes=[pltpu.VMEM((rows, width), jnp.bfloat16)],
        out_shape=[
            pltpu.VMEM((rows, share), jnp.float32),
            *[pltpu.VMEM((rows, width), jnp.bfloat16) for _ in late],
        ],
        compiler_params=room(2 * rows * width, 16 * rows * share),
        cost_estimate=pl.CostEstimate(
            flops=2 * rows * width * share * len(hops),
            transcendentals=0,
            bytes_accessed=2 * rows * width * len(hops),
        ),
        name="near",
    )(*[on_chip(p) for p in pieces], *[on_chip(p) for p in precond])


def far_kernel(routing, *refs, late, chips, parts):
    totals, refs = refs[:parts], refs[parts:]
    fars, refs = refs[: parts * len(late)], refs[parts * len(late) :]
    blocks, outs, acc = refs[: len(late)], refs[len(late) : -1], refs[-1]
    start = 0
    for part, total in enumerate(totals):
        span = slice(start, start + total.shape[0])
        start += total.shape[0]
        for i, (pair, block) in enumerate(zip(late, blocks)):
            _, here = hop_of(pair)

            @when(here)
            def _():
                before = total[...] if i == 0 else acc[span, :]
                acc[span, :] = before + contract(fars[part * len(late) + i][...], block[...])

    sending = jnp.dot(
        routing[...], acc[...].astype(jnp.bfloat16), preferred_element_type=jnp.float32
    ).astype(jnp.bfloat16)
    rows = sending.shape[0] // chips
    for chip in range(chips):
        outs[chip][...] = sending[chip * rows : (chip + 1) * rows, :]


def far_part(totals, routing, fars, blocks, late, chips):
    share = totals[0].shape[1]
    rows = sum(t.shape[0] for t in totals)
    sent = routing.shape[0] // chips
    operands = (routing, *totals, *sum(fars, []), *blocks)
    return pl.pallas_call(
        lambda *refs: far_kernel(*refs, late=late, chips=chips, parts=len(totals)),
        in_specs=[ON_CHIP] * len(operands),
        out_specs=[ON_CHIP] * chips,
        scratch_shapes=[pltpu.VMEM((rows, share), jnp.float32)],
        out_shape=[pltpu.VMEM((sent, share), jnp.bfloat16)] * chips,
        compiler_params=room(8 * routing.shape[0] * share, 8 * rows * share),
        cost_estimate=pl.CostEstimate(
            flops=2 * rows * blocks[0].size,
            transcendentals=0,
            bytes_accessed=2 * rows * blocks[0].shape[1],
        ),
        name="far",
    )(*[on_chip(o) for o in operands])


def contract(left, right):
    return lax.dot_general(
        left, right, (((1,), (1,)), ((), ())), preferred_element_type=jnp.float32
    )


def local(grads, scales, example_group, group_slot, inv_hess, queries):
    devices = lax.axis_size("dp")
    lanes = lax.axis_size("mp")
    chips = 1 << ((devices.bit_length() - 1) // 2)
    line = devices // chips
    per_lane = line // lanes
    width = inv_hess.shape[1]
    share = queries.shape[0] // lanes
    capacity = 2 * GRP_DEV // devices
    at_line = lax.axis_index("dp") // chips
    at_plane = lax.axis_index("dp") % chips

    def move(value, target):
        pairs = []
        for s in range(line):
            for t in range(chips):
                for m in range(lanes):
                    to = target(s, t, m)
                    if to is not None:
                        a, b, c = to
                        pairs.append(((s * chips + t) * lanes + m, (a * chips + b) * lanes + c))
        return lax.ppermute(value, AXES, pairs)

    def to_lane(value, hop):
        return move(value, lambda s, t, m: (s, t, m ^ hop))

    def to_plane(value, hop):
        return move(value, lambda s, t, m: (s, t ^ hop, m))

    def to_line(value, hop):
        return move(value, lambda s, t, m: (s ^ hop, t, m))

    mine, *theirs = precond_part(queries, inv_hess, lanes, 0, 1)
    block = mine
    for hop in range(1, lanes):
        block = block + to_lane(theirs[hop - 1], hop)
    block = block.astype(jnp.bfloat16)
    if line == 4:
        inside = (at_line == 1) | (at_line == 2)
        outward = {0: 2, 3: 1, 2: 3, 1: 0}
        early = move(block, lambda s, t, m: (outward[s], t, m))
        skip = move(block, lambda s, t, m: (s ^ 2, t, m) if s in (1, 2) else None)
        middle = move(block, lambda s, t, m: (s ^ 3, t, m) if s in (1, 2) else None)
        onward = jnp.where(inside, early, block)
        relay = move(onward, lambda s, t, m: (s ^ 1, t, m))
        nearer = {(0, 0): block, (1, 2): early, (2, None): skip}
        later = {(3, 1): relay, (None, 3): middle}
    else:
        nearer = {(0, 0): block}
        for hop in range(1, line):
            nearer[hop, hop] = to_line(block, hop)
        later = {(line - 1, line - 1): nearer.pop((line - 1, line - 1))}

    slot = group_slot.reshape(1, GRP_DEV)
    slots = [slot] + [to_plane(slot, hop) for hop in range(1, chips)]
    onehot = (
        jnp.arange(GRP_DEV, dtype=jnp.int32)[:, None] == example_group[0][None, :]
    ).astype(jnp.bfloat16)
    pieces = [None] * chips
    for peers in ((chips - 1,), tuple(range(1, chips - 1)), (0,)):
        made = group_part(grads, scales, onehot, peers, chips, per_lane, width)
        for hop, piece in zip(peers, made):
            pieces[hop] = to_plane(piece, hop) if hop else piece
    held = list(pieces)
    for hop in range(1, lanes):
        held += [to_lane(piece, hop) for piece in pieces]

    halves = ((0, *range(chips - 1, chips // 2, -1)), tuple(range(1, chips // 2 + 1)))
    sequence = halves[0] + halves[1]
    slot = jnp.concatenate([slots[hop] for hop in sequence], axis=0)
    owner, inside_owner = slot // GRP_DEV, slot % GRP_DEV
    source = jnp.bitwise_xor(jnp.array(sequence, jnp.int32), at_plane)[:, None]
    order = jnp.arange(GRP_DEV, dtype=jnp.int32)
    earlier = (owner[:, :, None] == owner[:, None, :]) & (order[None, :] < order[:, None])[None]
    rank = jnp.sum(earlier.astype(jnp.int32), axis=2)
    per_chip = chips * line * capacity
    toward = jnp.bitwise_xor(owner % chips, at_plane)
    row = toward * per_chip + (source * line + owner // chips) * capacity + rank
    rows = jnp.arange(chips * per_chip, dtype=jnp.int32)[:, None]
    routing = (rows == row.reshape(1, -1)).astype(jnp.bfloat16)
    kept = rows[:per_chip] == row.reshape(1, -1)
    meta = GRP_DEV + jnp.sum(
        jnp.where(kept, inside_owner.reshape(1, -1) - GRP_DEV, 0), axis=1, keepdims=True
    )
    meta = jnp.broadcast_to(meta, (per_chip, LANES)).astype(jnp.bfloat16)
    meta = meta.reshape(chips, line, capacity, LANES)

    late = tuple(later)
    totals, fars = [], []
    for some in halves:
        total, *parts = near_part(
            [held[lane * chips + hop] for lane in range(lanes) for hop in some],
            list(nearer.values()),
            tuple(nearer),
            late,
            len(some),
            lanes,
            per_lane,
            chips,
        )
        totals.append(total)
        fars.append(parts)
    sending = far_part(totals, routing, fars, list(later.values()), late, chips)
    whole = sending[0].astype(jnp.float32)
    for hop in range(1, chips):
        whole = whole + to_plane(sending[hop], hop).astype(jnp.float32)
    whole = whole.astype(jnp.bfloat16).reshape(chips, line, capacity, share)
    whole = jnp.concatenate([whole, meta], axis=3)
    final = []
    for hop in range(line):
        own = lax.dynamic_index_in_dim(whole, jnp.bitwise_xor(at_line, hop), 1, keepdims=False)
        own = own.reshape(chips * capacity, share + LANES)
        final.append(to_line(own, hop) if hop else own)
    final = jnp.concatenate(final, axis=0)
    chosen = (final[:, share:] == jnp.arange(LANES, dtype=jnp.bfloat16)[None, :]).astype(
        jnp.bfloat16
    )
    return lax.dot_general(
        chosen, final[:, :share], (((0,), (0,)), ((), ())), preferred_element_type=jnp.float32
    )


def solution(mesh):
    in_specs = (P("dp", "mp"), P("mp", "dp"), P("dp", None), P("dp"), P("mp", "dp"), P(None, "mp"))
    out_specs = P("dp", "mp")

    return jax.shard_map(local, mesh=mesh, in_specs=in_specs, out_specs=out_specs, check_vma=False)
```

```python
import jax
import jax.numpy as jnp
from jax import lax
from jax.experimental import pallas as pl
from jax.experimental.pallas import tpu as pltpu
from jax.sharding import PartitionSpec as P

QBLOCK = 128
GRP_DEV = 128
AXES = ("dp", "mp")
META = 8


ANYWHERE = pl.BlockSpec(memory_space=pl.ANY)
ON_CHIP = pl.BlockSpec(memory_space=pltpu.VMEM)


def room(*sizes):
    return pltpu.CompilerParams(vmem_limit_bytes=sum(sizes) + (4 << 20))


def on_chip(value):
    return pltpu.with_memory_space_constraint(value, pltpu.VMEM)


def precond_kernel(queries, inv_hess, mine, *refs, cut, blocks):
    theirs, (left, right, acc, sems) = refs[:-4], refs[-4:]
    width = right.shape[1]
    copies = []
    start = 0
    for i, depth in enumerate(blocks):
        span = pl.ds(start, depth)
        pair = (
            pltpu.make_async_copy(queries.at[:, span], left.at[:, span], sems.at[0, i]),
            pltpu.make_async_copy(
                inv_hess.at[span, pl.ds(cut * width, width)], right.at[span, :], sems.at[1, i]
            ),
        )
        for copy in pair:
            copy.start()
        copies.append((span, pair))
        start += depth
    for i, (span, pair) in enumerate(copies):
        for copy in pair:
            copy.wait()
        product = jnp.dot(left[:, span], right[span, :], preferred_element_type=jnp.float32)
        if i == 0:
            acc[...] = product
        else:
            acc[...] += product
    lane, share = lax.axis_index("mp"), mine.shape[0]
    mine[...] = acc[pl.ds(lane * share, share), :]
    for other, out in enumerate(theirs):
        first = jnp.bitwise_xor(lane, other + 1) * share
        out[...] = acc[pl.ds(first, share), :]


def precond_part(queries, inv_hess, lanes, cut, cuts):
    count, depth = queries.shape
    width = inv_hess.shape[1] // cuts
    share = count // lanes
    unit = depth // 16
    blocks = (unit, unit, 2 * unit, 4 * unit, 4 * unit, 4 * unit)
    return pl.pallas_call(
        lambda *refs: precond_kernel(*refs, cut=cut, blocks=blocks),
        in_specs=[ANYWHERE, ANYWHERE],
        out_specs=[ON_CHIP] * lanes,
        scratch_shapes=[
            pltpu.VMEM((count, depth), queries.dtype),
            pltpu.VMEM((depth, width), inv_hess.dtype),
            pltpu.VMEM((count, width), jnp.float32),
            pltpu.SemaphoreType.DMA((2, len(blocks))),
        ],
        out_shape=[pltpu.VMEM((share, width), jnp.float32)] * lanes,
        cost_estimate=pl.CostEstimate(
            flops=2 * count * depth * width,
            transcendentals=0,
            bytes_accessed=2 * (count * depth + depth * width),
        ),
        name="precond",
    )(queries, inv_hess)


def group_kernel(grads, scales, onehot, *refs, peers, chips, columns, width):
    outs, buffer, sems = refs[:-2], refs[-2], refs[-1]
    rows = buffer.shape[1]
    blocks = width // QBLOCK
    copies = []
    for out, peer in zip(outs, peers):
        for c in range(columns):
            column = c * chips + jnp.bitwise_xor(lax.axis_index("dp") % chips, peer)
            copy = pltpu.make_async_copy(
                grads.at[:, pl.ds(pl.multiple_of(column * width, width), width)],
                buffer.at[len(copies)],
                sems.at[len(copies)],
            )
            copy.start()
            copies.append((copy, out, column, c * width))
    for i, (copy, out, column, at) in enumerate(copies):
        copy.wait()
        turned = buffer[i].T.astype(jnp.float32).reshape(blocks, QBLOCK, rows)
        dequant = (turned * scales[column][:, None, :]).astype(jnp.bfloat16).reshape(width, rows)
        out[:, at : at + width] = lax.dot_general(
            onehot[...], dequant, (((1,), (1,)), ((), ())), preferred_element_type=jnp.float32
        ).astype(jnp.bfloat16)


def group_part(grads, scales, onehot, peers, chips, columns, width):
    rows = grads.shape[0]
    groups = onehot.shape[0]
    scales = scales.reshape(-1, width // QBLOCK, rows)
    shape = (groups, columns * width)
    count = len(peers) * columns
    return pl.pallas_call(
        lambda *refs: group_kernel(
            *refs, peers=peers, chips=chips, columns=columns, width=width
        ),
        in_specs=[ANYWHERE, ON_CHIP, ON_CHIP],
        out_specs=[ON_CHIP for _ in peers],
        scratch_shapes=[
            pltpu.VMEM((count, rows, width), grads.dtype),
            pltpu.SemaphoreType.DMA((count,)),
        ],
        out_shape=[pltpu.VMEM(shape, jnp.bfloat16) for _ in peers],
        cost_estimate=pl.CostEstimate(
            flops=2 * groups * rows * count * width,
            transcendentals=0,
            bytes_accessed=2 * rows * count * width,
        ),
    )(grads, on_chip(scales), on_chip(onehot))


def hop_of(pair):
    at_end, between = pair
    if at_end == between:
        return at_end, True
    where = lax.axis_index("dp") // (lax.axis_size("dp") // 4)
    inside = (where == 1) | (where == 2)
    if at_end is None:
        return between, inside
    if between is None:
        return at_end, jnp.logical_not(inside)
    return jnp.where(inside, between, at_end), True


def when(condition):
    return (lambda body: body()) if condition is True else pl.when(condition)


def near_kernel(*refs, hops, late, chips, lanes, per_lane, plane):
    pieces, refs = refs[: chips * lanes], refs[chips * lanes :]
    precond, total, left = refs[: len(hops)], refs[len(hops)], refs[-1]
    fars = refs[len(hops) + 1 : -1]
    rows, width = left.shape
    groups = rows // chips
    at_line = lax.axis_index("dp") // plane

    def lay(target, hop):
        source = jnp.bitwise_xor(at_line, hop)
        holder = jnp.bitwise_xor(source // per_lane, lax.axis_index("mp"))
        inner = source % per_lane
        for lane in range(lanes):
            for k in range(per_lane):

                @pl.when((holder == lane) & (inner == k))
                def _():
                    for chip in range(chips):
                        target[chip * groups : (chip + 1) * groups, :] = pieces[
                            lane * chips + chip
                        ][:groups, k * width : (k + 1) * width]

    for i, (pair, block) in enumerate(zip(hops, precond)):
        hop, here = hop_of(pair)

        @when(here)
        def _():
            lay(left, hop)
            part = contract(left[...], block[...])
            total[...] = part if i == 0 else total[...] + part

    for pair, far in zip(late, fars):
        hop, here = hop_of(pair)
        when(here)(lambda: lay(far, hop))


def near_part(pieces, precond, hops, late, chips, lanes, per_lane, plane):
    share, width = precond[0].shape
    rows = chips * (pieces[0].shape[0])
    return pl.pallas_call(
        lambda *refs: near_kernel(
            *refs,
            hops=hops,
            late=late,
            chips=chips,
            lanes=lanes,
            per_lane=per_lane,
            plane=plane,
        ),
        in_specs=[ON_CHIP] * (len(pieces) + len(precond)),
        out_specs=[ON_CHIP] * (1 + len(late)),
        scratch_shapes=[pltpu.VMEM((rows, width), jnp.bfloat16)],
        out_shape=[
            pltpu.VMEM((rows, share), jnp.float32),
            *[pltpu.VMEM((rows, width), jnp.bfloat16) for _ in late],
        ],
        compiler_params=room(2 * rows * width, 16 * rows * share),
        cost_estimate=pl.CostEstimate(
            flops=2 * rows * width * share * len(hops),
            transcendentals=0,
            bytes_accessed=2 * rows * width * len(hops),
        ),
        name="near",
    )(*[on_chip(p) for p in pieces], *[on_chip(p) for p in precond])


def far_kernel(routing, *refs, late, chips, parts):
    totals, refs = refs[:parts], refs[parts:]
    fars, refs = refs[: parts * len(late)], refs[parts * len(late) :]
    blocks, outs, acc = refs[: len(late)], refs[len(late) : -1], refs[-1]
    start = 0
    for part, total in enumerate(totals):
        span = slice(start, start + total.shape[0])
        start += total.shape[0]
        acc[span, :] = total[...]
        for i, (pair, block) in enumerate(zip(late, blocks)):
            _, here = hop_of(pair)

            @when(here)
            def _():
                acc[span, :] += contract(fars[part * len(late) + i][...], block[...])

    sending = jnp.dot(
        routing[...], acc[...].astype(jnp.bfloat16), preferred_element_type=jnp.float32
    ).astype(jnp.bfloat16)
    rows = sending.shape[0] // chips
    for chip in range(chips):
        outs[chip][...] = sending[chip * rows : (chip + 1) * rows, :]


def far_part(totals, routing, fars, blocks, late, chips):
    share = totals[0].shape[1]
    rows = sum(t.shape[0] for t in totals)
    sent = routing.shape[0] // chips
    operands = (routing, *totals, *sum(fars, []), *blocks)
    return pl.pallas_call(
        lambda *refs: far_kernel(*refs, late=late, chips=chips, parts=len(totals)),
        in_specs=[ON_CHIP] * len(operands),
        out_specs=[ON_CHIP] * chips,
        scratch_shapes=[pltpu.VMEM((rows, share), jnp.float32)],
        out_shape=[pltpu.VMEM((sent, share), jnp.bfloat16)] * chips,
        compiler_params=room(8 * routing.shape[0] * share, 8 * rows * share),
        cost_estimate=pl.CostEstimate(
            flops=2 * rows * blocks[0].size,
            transcendentals=0,
            bytes_accessed=2 * rows * blocks[0].shape[1],
        ),
        name="far",
    )(*[on_chip(o) for o in operands])


def contract(left, right):
    return lax.dot_general(
        left, right, (((1,), (1,)), ((), ())), preferred_element_type=jnp.float32
    )


def local(grads, scales, example_group, group_slot, inv_hess, queries):
    devices = lax.axis_size("dp")
    lanes = lax.axis_size("mp")
    chips = 1 << ((devices.bit_length() - 1) // 2)
    line = devices // chips
    per_lane = line // lanes
    width = inv_hess.shape[1]
    share = queries.shape[0] // lanes
    capacity = 2 * GRP_DEV // devices
    at_line = lax.axis_index("dp") // chips
    at_plane = lax.axis_index("dp") % chips

    def move(value, target):
        pairs = []
        for s in range(line):
            for t in range(chips):
                for m in range(lanes):
                    to = target(s, t, m)
                    if to is not None:
                        a, b, c = to
                        pairs.append(((s * chips + t) * lanes + m, (a * chips + b) * lanes + c))
        return lax.ppermute(value, AXES, pairs)

    def to_lane(value, hop):
        return move(value, lambda s, t, m: (s, t, m ^ hop))

    def to_plane(value, hop):
        return move(value, lambda s, t, m: (s, t ^ hop, m))

    def to_line(value, hop):
        return move(value, lambda s, t, m: (s ^ hop, t, m))

    mine, *theirs = precond_part(queries, inv_hess, lanes, 0, 1)
    block = mine
    for hop in range(1, lanes):
        block = block + to_lane(theirs[hop - 1], hop)
    block = block.astype(jnp.bfloat16)
    if line == 4:
        early = move(block, lambda s, t, m: ((2, 0, 3, 1)[s], t, m))
        skip = move(block, lambda s, t, m: ((1, 3, 0, 2)[s], t, m))
        relay = move(early, lambda s, t, m: (s ^ 1, t, m) if s in (1, 2) else None)
        middle = move(block, lambda s, t, m: (s ^ 3, t, m) if s in (1, 2) else None)
        nearer = {(0, 0): block, (1, 2): early, (2, 1): skip}
        later = {(3, None): relay, (None, 3): middle}
    else:
        nearer = {(0, 0): block}
        for hop in range(1, line):
            nearer[hop, hop] = to_line(block, hop)
        later = {(line - 1, line - 1): nearer.pop((line - 1, line - 1))}

    slot = group_slot.reshape(1, GRP_DEV)
    slots = [slot] + [to_plane(slot, hop) for hop in range(1, chips)]
    onehot = (
        jnp.arange(GRP_DEV, dtype=jnp.int32)[:, None] == example_group[0][None, :]
    ).astype(jnp.bfloat16)
    pieces = [None] * chips
    for peers in ((chips - 1,), tuple(range(1, chips - 1)), (0,)):
        made = group_part(grads, scales, onehot, peers, chips, per_lane, width)
        for hop, piece in zip(peers, made):
            pieces[hop] = to_plane(piece, hop) if hop else piece
    held = list(pieces)
    for hop in range(1, lanes):
        held += [to_lane(piece, hop) for piece in pieces]

    halves = ((0, *range(chips - 1, chips // 2, -1)), tuple(range(1, chips // 2 + 1)))
    sequence = halves[0] + halves[1]
    slot = jnp.concatenate([slots[hop] for hop in sequence], axis=0)
    owner, inside_owner = slot // GRP_DEV, slot % GRP_DEV
    source = jnp.bitwise_xor(jnp.array(sequence, jnp.int32), at_plane)[:, None]
    order = jnp.arange(GRP_DEV, dtype=jnp.int32)
    earlier = (owner[:, :, None] == owner[:, None, :]) & (order[None, :] < order[:, None])[None]
    rank = jnp.sum(earlier.astype(jnp.int32), axis=2)
    per_chip = chips * line * capacity
    toward = jnp.bitwise_xor(owner % chips, at_plane)
    row = toward * per_chip + (source * line + owner // chips) * capacity + rank
    rows = jnp.arange(chips * per_chip, dtype=jnp.int32)[:, None]
    routing = (rows == row.reshape(1, -1)).astype(jnp.bfloat16)
    kept = rows[:per_chip] == row.reshape(1, -1)
    meta = GRP_DEV + jnp.sum(jnp.where(kept, inside_owner.reshape(1, -1) - GRP_DEV, 0), axis=1)
    meta = meta.astype(jnp.bfloat16).reshape(chips, line, capacity)
    meta = meta.transpose(1, 0, 2).reshape(line, 1, chips * capacity)
    meta = jnp.pad(meta, ((0, 0), (0, META - 1), (0, share - chips * capacity)))

    late = tuple(later)
    totals, fars = [], []
    for some in halves:
        total, *parts = near_part(
            [held[lane * chips + hop] for lane in range(lanes) for hop in some],
            list(nearer.values()),
            tuple(nearer),
            late,
            len(some),
            lanes,
            per_lane,
            chips,
        )
        totals.append(total)
        fars.append(parts)
    sending = far_part(totals, routing, fars, list(later.values()), late, chips)
    whole = sending[0].astype(jnp.float32)
    for hop in range(1, chips):
        whole = whole + to_plane(sending[hop], hop).astype(jnp.float32)
    whole = whole.astype(jnp.bfloat16).reshape(chips, line, capacity, share)
    final, targets = [], []
    for hop in range(line):
        owner = jnp.bitwise_xor(at_line, hop)
        own = lax.dynamic_index_in_dim(whole, owner, 1, keepdims=False)
        target = lax.dynamic_index_in_dim(meta, owner, 0, keepdims=False)
        own = jnp.concatenate([own.reshape(chips * capacity, share), target], axis=0)
        got = to_line(own, hop) if hop else own
        final.append(got[: chips * capacity])
        targets.append(got[chips * capacity : chips * capacity + 1, : chips * capacity])
    final = jnp.concatenate(final, axis=0)
    targets = jnp.concatenate(targets, axis=1)
    chosen = (jnp.arange(GRP_DEV, dtype=jnp.bfloat16)[:, None] == targets).astype(jnp.bfloat16)
    return jnp.dot(chosen, final, preferred_element_type=jnp.float32)


def solution(mesh):
    in_specs = (P("dp", "mp"), P("mp", "dp"), P("dp", None), P("dp"), P("mp", "dp"), P(None, "mp"))
    out_specs = P("dp", "mp")

    return jax.shard_map(local, mesh=mesh, in_specs=in_specs, out_specs=out_specs, check_vma=False)
```

```python
import jax
import jax.numpy as jnp
from jax import lax
from jax.experimental import pallas as pl
from jax.experimental.pallas import tpu as pltpu
from jax.sharding import PartitionSpec as P

QBLOCK = 128
GRP_DEV = 128
AXES = ("dp", "mp")
META = 8


ANYWHERE = pl.BlockSpec(memory_space=pl.ANY)
ON_CHIP = pl.BlockSpec(memory_space=pltpu.VMEM)


def room(*sizes):
    return pltpu.CompilerParams(vmem_limit_bytes=sum(sizes) + (4 << 20))


def on_chip(value):
    return pltpu.with_memory_space_constraint(value, pltpu.VMEM)


def precond_kernel(queries, inv_hess, mine, *refs, cut, blocks):
    theirs, (left, right, acc, sems) = refs[:-4], refs[-4:]
    width = right.shape[1]
    copies = []
    start = 0
    for i, depth in enumerate(blocks):
        span = pl.ds(start, depth)
        pair = (
            pltpu.make_async_copy(queries.at[:, span], left.at[:, span], sems.at[0, i]),
            pltpu.make_async_copy(
                inv_hess.at[span, pl.ds(cut * width, width)], right.at[span, :], sems.at[1, i]
            ),
        )
        for copy in pair:
            copy.start()
        copies.append((span, pair))
        start += depth
    for i, (span, pair) in enumerate(copies):
        for copy in pair:
            copy.wait()
        product = jnp.dot(left[:, span], right[span, :], preferred_element_type=jnp.float32)
        if i == 0:
            acc[...] = product
        else:
            acc[...] += product
    lane, share = lax.axis_index("mp"), mine.shape[0]
    mine[...] = acc[pl.ds(lane * share, share), :]
    for other, out in enumerate(theirs):
        first = jnp.bitwise_xor(lane, other + 1) * share
        out[...] = acc[pl.ds(first, share), :]


def precond_part(queries, inv_hess, lanes, cut, cuts):
    count, depth = queries.shape
    width = inv_hess.shape[1] // cuts
    share = count // lanes
    unit = depth // 16
    blocks = (unit, unit, 2 * unit, 4 * unit, 4 * unit, 4 * unit)
    return pl.pallas_call(
        lambda *refs: precond_kernel(*refs, cut=cut, blocks=blocks),
        in_specs=[ANYWHERE, ANYWHERE],
        out_specs=[ON_CHIP] * lanes,
        scratch_shapes=[
            pltpu.VMEM((count, depth), queries.dtype),
            pltpu.VMEM((depth, width), inv_hess.dtype),
            pltpu.VMEM((count, width), jnp.float32),
            pltpu.SemaphoreType.DMA((2, len(blocks))),
        ],
        out_shape=[pltpu.VMEM((share, width), jnp.float32)] * lanes,
        cost_estimate=pl.CostEstimate(
            flops=2 * count * depth * width,
            transcendentals=0,
            bytes_accessed=2 * (count * depth + depth * width),
        ),
        name="precond",
    )(queries, inv_hess)


def group_kernel(grads, scales, onehot, *refs, peers, chips, columns, width):
    outs, buffer, sems = refs[:-2], refs[-2], refs[-1]
    rows = buffer.shape[1]
    copies = []
    for out, peer in zip(outs, peers):
        for c in range(columns):
            column = c * chips + jnp.bitwise_xor(lax.axis_index("dp") % chips, peer)
            cut = width if copies else width // 2
            for first in range(0, width, cut):
                at = len(copies)
                slot = buffer.at[c + columns * peers.index(peer), :, pl.ds(first, cut)]
                start = pl.multiple_of(column * width + first, cut)
                copy = pltpu.make_async_copy(grads.at[:, pl.ds(start, cut)], slot, sems.at[at])
                copy.start()
                copies.append((copy, slot, out, column, first, cut, c * width + first))
    for copy, slot, out, column, first, cut, at in copies:
        copy.wait()
        blocks = cut // QBLOCK
        turned = slot[...].T.astype(jnp.float32).reshape(blocks, QBLOCK, rows)
        steps = scales[column][first // QBLOCK : first // QBLOCK + blocks, :]
        dequant = (turned * steps[:, None, :]).astype(jnp.bfloat16).reshape(cut, rows)
        out[:, at : at + cut] = lax.dot_general(
            onehot[...], dequant, (((1,), (1,)), ((), ())), preferred_element_type=jnp.float32
        ).astype(jnp.bfloat16)


def group_part(grads, scales, onehot, peers, chips, columns, width):
    rows = grads.shape[0]
    groups = onehot.shape[0]
    scales = scales.reshape(-1, width // QBLOCK, rows)
    shape = (groups, columns * width)
    count = len(peers) * columns
    return pl.pallas_call(
        lambda *refs: group_kernel(
            *refs, peers=peers, chips=chips, columns=columns, width=width
        ),
        in_specs=[ANYWHERE, ON_CHIP, ON_CHIP],
        out_specs=[ON_CHIP for _ in peers],
        scratch_shapes=[
            pltpu.VMEM((count, rows, width), grads.dtype),
            pltpu.SemaphoreType.DMA((count + 1,)),
        ],
        out_shape=[pltpu.VMEM(shape, jnp.bfloat16) for _ in peers],
        cost_estimate=pl.CostEstimate(
            flops=2 * groups * rows * count * width,
            transcendentals=0,
            bytes_accessed=2 * rows * count * width,
        ),
    )(grads, on_chip(scales), on_chip(onehot))


def hop_of(pair):
    at_end, between = pair
    if at_end == between:
        return at_end, True
    where = lax.axis_index("dp") // (lax.axis_size("dp") // 4)
    inside = (where == 1) | (where == 2)
    if at_end is None:
        return between, inside
    if between is None:
        return at_end, jnp.logical_not(inside)
    return jnp.where(inside, between, at_end), True


def when(condition):
    return (lambda body: body()) if condition is True else pl.when(condition)


def near_kernel(*refs, hops, late, chips, lanes, per_lane, plane):
    pieces, refs = refs[: chips * lanes], refs[chips * lanes :]
    precond, total, left = refs[: len(hops)], refs[len(hops)], refs[-1]
    fars = refs[len(hops) + 1 : -1]
    rows, width = left.shape
    groups = rows // chips
    at_line = lax.axis_index("dp") // plane

    def lay(target, hop):
        source = jnp.bitwise_xor(at_line, hop)
        holder = jnp.bitwise_xor(source // per_lane, lax.axis_index("mp"))
        inner = source % per_lane
        for lane in range(lanes):
            for k in range(per_lane):

                @pl.when((holder == lane) & (inner == k))
                def _():
                    for chip in range(chips):
                        target[chip * groups : (chip + 1) * groups, :] = pieces[
                            lane * chips + chip
                        ][:groups, k * width : (k + 1) * width]

    for i, (pair, block) in enumerate(zip(hops, precond)):
        hop, here = hop_of(pair)

        @when(here)
        def _():
            lay(left, hop)
            part = contract(left[...], block[...])
            total[...] = part if i == 0 else total[...] + part

    for pair, far in zip(late, fars):
        hop, here = hop_of(pair)
        when(here)(lambda: lay(far, hop))


def near_part(pieces, precond, hops, late, chips, lanes, per_lane, plane):
    share, width = precond[0].shape
    rows = chips * (pieces[0].shape[0])
    return pl.pallas_call(
        lambda *refs: near_kernel(
            *refs,
            hops=hops,
            late=late,
            chips=chips,
            lanes=lanes,
            per_lane=per_lane,
            plane=plane,
        ),
        in_specs=[ON_CHIP] * (len(pieces) + len(precond)),
        out_specs=[ON_CHIP] * (1 + len(late)),
        scratch_shapes=[pltpu.VMEM((rows, width), jnp.bfloat16)],
        out_shape=[
            pltpu.VMEM((rows, share), jnp.float32),
            *[pltpu.VMEM((rows, width), jnp.bfloat16) for _ in late],
        ],
        compiler_params=room(2 * rows * width, 16 * rows * share),
        cost_estimate=pl.CostEstimate(
            flops=2 * rows * width * share * len(hops),
            transcendentals=0,
            bytes_accessed=2 * rows * width * len(hops),
        ),
        name="near",
    )(*[on_chip(p) for p in pieces], *[on_chip(p) for p in precond])


def far_kernel(routing, *refs, late, chips, parts):
    totals, refs = refs[:parts], refs[parts:]
    fars, refs = refs[: parts * len(late)], refs[parts * len(late) :]
    blocks, outs, acc = refs[: len(late)], refs[len(late) : -1], refs[-1]
    start = 0
    for part, total in enumerate(totals):
        span = slice(start, start + total.shape[0])
        start += total.shape[0]
        acc[span, :] = total[...]
        for i, (pair, block) in enumerate(zip(late, blocks)):
            _, here = hop_of(pair)

            @when(here)
            def _():
                acc[span, :] += contract(fars[part * len(late) + i][...], block[...])

    sending = jnp.dot(
        routing[...], acc[...].astype(jnp.bfloat16), preferred_element_type=jnp.float32
    ).astype(jnp.bfloat16)
    rows = sending.shape[0] // chips
    for chip in range(chips):
        outs[chip][...] = sending[chip * rows : (chip + 1) * rows, :]


def far_part(totals, routing, fars, blocks, late, chips):
    share = totals[0].shape[1]
    rows = sum(t.shape[0] for t in totals)
    sent = routing.shape[0] // chips
    operands = (routing, *totals, *sum(fars, []), *blocks)
    return pl.pallas_call(
        lambda *refs: far_kernel(*refs, late=late, chips=chips, parts=len(totals)),
        in_specs=[ON_CHIP] * len(operands),
        out_specs=[ON_CHIP] * chips,
        scratch_shapes=[pltpu.VMEM((rows, share), jnp.float32)],
        out_shape=[pltpu.VMEM((sent, share), jnp.bfloat16)] * chips,
        compiler_params=room(8 * routing.shape[0] * share, 8 * rows * share),
        cost_estimate=pl.CostEstimate(
            flops=2 * rows * blocks[0].size,
            transcendentals=0,
            bytes_accessed=2 * rows * blocks[0].shape[1],
        ),
        name="far",
    )(*[on_chip(o) for o in operands])


def contract(left, right):
    return lax.dot_general(
        left, right, (((1,), (1,)), ((), ())), preferred_element_type=jnp.float32
    )


def local(grads, scales, example_group, group_slot, inv_hess, queries):
    devices = lax.axis_size("dp")
    lanes = lax.axis_size("mp")
    chips = 1 << ((devices.bit_length() - 1) // 2)
    line = devices // chips
    per_lane = line // lanes
    width = inv_hess.shape[1]
    share = queries.shape[0] // lanes
    capacity = 2 * GRP_DEV // devices
    at_line = lax.axis_index("dp") // chips
    at_plane = lax.axis_index("dp") % chips

    def move(value, target):
        pairs = []
        for s in range(line):
            for t in range(chips):
                for m in range(lanes):
                    to = target(s, t, m)
                    if to is not None:
                        a, b, c = to
                        pairs.append(((s * chips + t) * lanes + m, (a * chips + b) * lanes + c))
        return lax.ppermute(value, AXES, pairs)

    def to_lane(value, hop):
        return move(value, lambda s, t, m: (s, t, m ^ hop))

    def to_plane(value, hop):
        return move(value, lambda s, t, m: (s, t ^ hop, m))

    def to_line(value, hop):
        return move(value, lambda s, t, m: (s ^ hop, t, m))

    mine, *theirs = precond_part(queries, inv_hess, lanes, 0, 1)
    block = mine
    for hop in range(1, lanes):
        block = block + to_lane(theirs[hop - 1], hop)
    block = block.astype(jnp.bfloat16)
    if line == 4:
        early = move(block, lambda s, t, m: ((2, 0, 3, 1)[s], t, m))
        skip = move(block, lambda s, t, m: ((1, 3, 0, 2)[s], t, m))
        relay = move(early, lambda s, t, m: (s ^ 1, t, m) if s in (1, 2) else None)
        middle = move(block, lambda s, t, m: (s ^ 3, t, m) if s in (1, 2) else None)
        nearer = {(0, 0): block, (1, 2): early, (2, 1): skip}
        later = {(3, None): relay, (None, 3): middle}
    else:
        nearer = {(0, 0): block}
        for hop in range(1, line):
            nearer[hop, hop] = to_line(block, hop)
        later = {(line - 1, line - 1): nearer.pop((line - 1, line - 1))}

    slot = group_slot.reshape(1, GRP_DEV)
    slots = [slot] + [to_plane(slot, hop) for hop in range(1, chips)]
    onehot = (
        jnp.arange(GRP_DEV, dtype=jnp.int32)[:, None] == example_group[0][None, :]
    ).astype(jnp.bfloat16)
    pieces = [None] * chips
    for peers in ((chips - 1,), tuple(range(1, chips - 1)), (0,)):
        made = group_part(grads, scales, onehot, peers, chips, per_lane, width)
        for hop, piece in zip(peers, made):
            pieces[hop] = to_plane(piece, hop) if hop else piece
    held = list(pieces)
    for hop in range(1, lanes):
        held += [to_lane(piece, hop) for piece in pieces]

    halves = ((0, *range(chips - 1, chips // 2, -1)), tuple(range(1, chips // 2 + 1)))
    sequence = halves[0] + halves[1]
    slot = jnp.concatenate([slots[hop] for hop in sequence], axis=0)
    owner, inside_owner = slot // GRP_DEV, slot % GRP_DEV
    source = jnp.bitwise_xor(jnp.array(sequence, jnp.int32), at_plane)[:, None]
    order = jnp.arange(GRP_DEV, dtype=jnp.int32)
    earlier = (owner[:, :, None] == owner[:, None, :]) & (order[None, :] < order[:, None])[None]
    rank = jnp.sum(earlier.astype(jnp.int32), axis=2)
    per_chip = chips * line * capacity
    toward = jnp.bitwise_xor(owner % chips, at_plane)
    row = toward * per_chip + (source * line + owner // chips) * capacity + rank
    rows = jnp.arange(chips * per_chip, dtype=jnp.int32)[:, None]
    routing = (rows == row.reshape(1, -1)).astype(jnp.bfloat16)
    kept = rows[:per_chip] == row.reshape(1, -1)
    meta = GRP_DEV + jnp.sum(jnp.where(kept, inside_owner.reshape(1, -1) - GRP_DEV, 0), axis=1)
    meta = meta.astype(jnp.bfloat16).reshape(chips, line, capacity)
    meta = meta.transpose(1, 0, 2).reshape(line, 1, chips * capacity)
    meta = jnp.pad(meta, ((0, 0), (0, META - 1), (0, share - chips * capacity)))

    late = tuple(later)
    totals, fars = [], []
    for some in halves:
        total, *parts = near_part(
            [held[lane * chips + hop] for lane in range(lanes) for hop in some],
            list(nearer.values()),
            tuple(nearer),
            late,
            len(some),
            lanes,
            per_lane,
            chips,
        )
        totals.append(total)
        fars.append(parts)
    sending = far_part(totals, routing, fars, list(later.values()), late, chips)
    whole = sending[0].astype(jnp.float32)
    for hop in range(1, chips):
        whole = whole + to_plane(sending[hop], hop).astype(jnp.float32)
    whole = whole.astype(jnp.bfloat16).reshape(chips, line, capacity, share)
    final, targets = [], []
    for hop in range(line):
        owner = jnp.bitwise_xor(at_line, hop)
        own = lax.dynamic_index_in_dim(whole, owner, 1, keepdims=False)
        target = lax.dynamic_index_in_dim(meta, owner, 0, keepdims=False)
        own = jnp.concatenate([own.reshape(chips * capacity, share), target], axis=0)
        got = to_line(own, hop) if hop else own
        final.append(got[: chips * capacity])
        targets.append(got[chips * capacity : chips * capacity + 1, : chips * capacity])
    final = jnp.concatenate(final, axis=0)
    targets = jnp.concatenate(targets, axis=1)
    chosen = (jnp.arange(GRP_DEV, dtype=jnp.bfloat16)[:, None] == targets).astype(jnp.bfloat16)
    return jnp.dot(chosen, final, preferred_element_type=jnp.float32)


def solution(mesh):
    in_specs = (P("dp", "mp"), P("mp", "dp"), P("dp", None), P("dp"), P("mp", "dp"), P(None, "mp"))
    out_specs = P("dp", "mp")

    return jax.shard_map(local, mesh=mesh, in_specs=in_specs, out_specs=out_specs, check_vma=False)
```
